768 devices in a mesh: sub: 96 (over y, z), grp: 8 (over x, core).
Axes of the slice: x: 4, y: 8, z: 12, core: 2. Of those that a mesh axis runs over, the one named last changes fastest.
Arguments:
- rhs: float32 [96, 8, 64, 128], P('sub', 'grp')
- guess: float32 [96, 8, 64, 128], P('sub', 'grp'), may hold values from -6 to 6
- blocks: bfloat16 [96, 8, 64, 64, 128], P('sub', 'grp')
- valve: int32 [96, 8, 128], P('sub', 'grp'), may hold values 0 or 1
- jscale: float32 [96, 8, 64, 128], P('sub', 'grp'), may hold values from 0.1 to 0.4
- prolong: float32 [96, 8, 64, 128], P('sub', 'grp'), may hold values from -0.75 to 0.75
- agg_map: int32 [96, 8, 128], P('sub', 'grp'), may hold values from 0 to 47
- cdiag: float32 [36864], P(('sub', 'grp')), may hold values from 0.5 to 2
- coff: bfloat16 [36864, 36864], P(('sub', 'grp')), may hold values from -0.125 to 0.125
- send_rows: int32 [96, 8, 2, 128], P('sub', 'grp'), may hold values from 0 to 127
- recv_rows: int32 [96, 8, 2, 128], P('sub', 'grp'), may hold values from 0 to 127
- live_counts: int32 [96, 8, 2], P('sub', 'grp'), may hold values from 32 to 128, as said below
Outputs:
- solution: float32 [96, 8, 64, 128], P('sub', 'grp')
- next_basis: float32 [96, 8, 64, 128], P('sub', 'grp')
The draws below stay inside these ranges and needn't reach their ends.
Inputs may be any that keep to these rules, and one draw needn't show every extreme that they name: `send_rows`: block numbers of the sending subdomain. `recv_rows`: block numbers of the receiving subdomain; several slots may name one block. `live_counts`: some subdomain has every slot live in both lists. `agg_map`: aggregates may be empty.
All inputs are finite; a program needn't handle non-finite values. No bound on the sum of `valve` on one device may be relied on, other than what follows from the above.
Results may differ from the reference program's by a relative error of at most 0.003.
Values may be sent and summed in bfloat16 or wider, within the bound.
A program may use at most 32 MiB of HBM per device.

```python
import math
import jax
import jax.numpy as jnp
from jax import lax

BS = 64
NB = 128
SLOTS = 128
CPD = 48
NC = 36864
ITERS = 2
N_SUB = 96
N_GRP = 8


def draw_rhs(key, part):
    shape = (N_SUB, N_GRP, BS, NB)
    rise = 1.0 + 2.0 * jnp.arange(N_SUB, dtype=jnp.float32) / max(N_SUB - 1, 1)
    base = jax.random.normal(key, shape, jnp.float32)
    return base * rise[:, None, None, None]


def draw_blocks(key, part):
    shape = (N_SUB, N_GRP, BS, BS, NB)
    places = jnp.arange(BS, dtype=jnp.int32)
    unit = (places[:, None] == places[None, :]).astype(jnp.float32)[None, None, :, :, None]
    noise = jax.random.normal(key, shape, jnp.float32)
    noise = noise * (2.0 / BS ** 0.5)
    return (4.0 * unit + noise * (1.0 - unit)).astype(jnp.bfloat16)


def draw_live_counts(key, part):
    counts = jax.random.randint(key, (N_SUB, N_GRP, 2), NB // 4, NB + 1, dtype=jnp.int32)
    return counts.at[1, 0, :].set(NB)


def place_ends(drawn, stream_key, low, high):
    extent = drawn.shape
    place = [jax.random.randint(jax.random.fold_in(stream_key, axis), (), 0, extent[axis]) for axis in range(len(extent))]
    drawn = drawn.at[tuple(place)].set(low)
    longest = extent.index(max(extent))
    place[longest] = (place[longest] + 1) % extent[longest]
    return drawn.at[tuple(place)].set(high)


def with_spikes(drawn, key, source, target, blocks, factor):
    def block_of(dim):
        return (jnp.arange(drawn.shape[dim]) // (drawn.shape[dim] // blocks)).reshape((-1,) + (1,) * (drawn.ndim - 1 - dim))

    one_side = jax.random.permutation(key, blocks)[block_of(target)]
    other_side = (block_of(target) + blocks // 2) % blocks
    return jnp.where((block_of(source) == one_side) | (block_of(source) == other_side), factor * drawn, drawn)


def steps_of(rng, shape, split, low, top_value):
    loudness = 1.0
    for axis_at, parts in split:
        draws = jax.random.uniform(jax.random.fold_in(jax.random.fold_in(rng, 6), axis_at), (parts,), jnp.float32, low / len(split), top_value / len(split))
        loudness = loudness * jnp.repeat(jnp.exp(draws), shape[axis_at] // parts).reshape((-1,) + (1,) * (len(shape) - 1 - axis_at))
    return loudness


def gaussian(rng, shape, deviation, most, split=(), kind=jnp.bfloat16):
    factor_of = steps_of(rng, shape, split, -0.22, 0.18) if split else 1.0
    drawn = jax.random.normal(rng, shape, jnp.float32) * deviation * factor_of
    return jnp.minimum(jnp.maximum(drawn, -most), most).astype(kind)


def heavy_noise(key, shape, width, most, cuts, heavy, kind=jnp.bfloat16):
    values = width * jax.random.normal(key, shape, jnp.float32)
    if cuts:
        values = values * steps_of(key, shape, cuts, -0.22, 0.18)
    return jnp.clip(with_spikes(values, jax.random.fold_in(key, 3), *heavy), -most, most).astype(kind)


def setup_inputs(seed: int = 0) -> dict:
    keys = jax.random.split(jax.random.key(seed), 13)
    return {
        "rhs": draw_rhs(jax.random.fold_in(keys[12], 71), 0),
        "guess": gaussian(keys[1], (N_SUB, N_GRP, BS, NB), 1.0, 6.0, ((0, 96), (1, 8)), jnp.float32),
        "blocks": draw_blocks(jax.random.fold_in(keys[12], 71), 0),
        "valve": place_ends((jax.random.randint(keys[3], (N_SUB, N_GRP, NB), 0, 3) < 1).astype(jnp.int32), jax.random.fold_in(keys[3], 1), 0, 1),
        "jscale": jnp.clip(jnp.exp(math.log(0.4) - 1.3862944 * jax.random.uniform(keys[4], (N_SUB, N_GRP, BS, NB), jnp.float32) ** steps_of(keys[4], (N_SUB, N_GRP, BS, NB), ((0, 96), (1, 8)), -0.2, 0.2)), 0.1, 0.4),
        "prolong": gaussian(keys[5], (N_SUB, N_GRP, BS, NB), BS ** -0.5, 0.75, ((0, 96), (1, 8)), jnp.float32),
        "agg_map": place_ends(jax.random.randint(keys[6], (N_SUB, N_GRP, NB), 0, CPD), jax.random.fold_in(keys[6], 1), 0, CPD - 1).astype(jnp.int32),
        "cdiag": jnp.clip(jnp.exp(math.log(2.0) - 1.3862944 * jax.random.uniform(keys[7], (NC,), jnp.float32) ** steps_of(keys[7], (NC,), ((0, 768),), -0.2, 0.2)), 0.5, 2.0),
        "coff": heavy_noise(keys[8], (NC, NC), NC ** -0.5, 0.125, ((0, 768),), (1, 0, 768, 6.0)),
        "send_rows": place_ends(jax.random.randint(keys[9], (N_SUB, N_GRP, 2, SLOTS), 0, NB), jax.random.fold_in(keys[9], 1), 0, NB - 1).astype(jnp.int32),
        "recv_rows": place_ends(jax.random.randint(keys[10], (N_SUB, N_GRP, 2, SLOTS), 0, NB), jax.random.fold_in(keys[10], 1), 0, NB - 1).astype(jnp.int32),
        "live_counts": draw_live_counts(jax.random.fold_in(keys[12], 71), 0),
    }


penalty_gain = 3.0
coupling = 0.5

def received(packed, recv_rows, live_counts, side):
    slots = jnp.arange(recv_rows.shape[3], dtype=jnp.int32)
    places = jnp.arange(NB, dtype=jnp.int32)
    live = slots[None, None, :] < live_counts[:, :, side][:, :, None]
    onehot = ((recv_rows[:, :, side, :, None] == places[None, None, None, :]) & live[:, :, :, None]).astype(jnp.float32)
    return jnp.einsum('sgik,sgkb->sgib', packed, onehot, precision=lax.Precision.HIGHEST)

def operate(field, blocks, valve, send_rows, recv_rows, live_counts):
    out = jnp.einsum('sgijb,sgjb->sgib', blocks.astype(jnp.float32), field, precision=lax.Precision.HIGHEST)
    out = out + penalty_gain * valve.astype(jnp.float32)[:, :, None, :] * field
    shape = (field.shape[0], field.shape[1], field.shape[2], send_rows.shape[3])
    upward = jnp.take_along_axis(field, jnp.broadcast_to(send_rows[:, :, 0][:, :, None, :], shape), axis=3)
    downward = jnp.take_along_axis(field, jnp.broadcast_to(send_rows[:, :, 1][:, :, None, :], shape), axis=3)
    below = jnp.concatenate([jnp.zeros_like(upward[:1]), upward[:-1]], axis=0)
    above = jnp.concatenate([downward[1:], jnp.zeros_like(downward[:1])], axis=0)
    return out - coupling * (received(below, recv_rows, live_counts, 0) + received(above, recv_rows, live_counts, 1))

def precondition(field, jscale, prolong, agg_map, cdiag, coff):
    weighted = lax.optimization_barrier(jnp.sum(prolong * field, axis=2))
    agg_sel = (agg_map[:, :, :, None] == jnp.arange(CPD, dtype=jnp.int32)[None, None, None, :]).astype(jnp.float32)
    coarse = jnp.einsum('sgb,sgbc->sgc', weighted, agg_sel, precision=lax.Precision.HIGHEST)
    flat = coarse.reshape(NC)
    coarse_half = flat.astype(jnp.bfloat16)
    coarse_sol = cdiag * flat + jnp.dot(coff, coarse_half, preferred_element_type=jnp.float32)
    coarse_sol = coarse_sol.reshape(coarse.shape)
    spread = jnp.einsum('sgbc,sgc->sgb', agg_sel, coarse_sol, precision=lax.Precision.HIGHEST)
    return jscale * field + prolong * spread[:, :, None, :]

def solve_small(gram, target):
    count = target.shape[0]
    matrix = [[gram[row, col] for col in range(count)] for row in range(count)]
    vector = [target[row] for row in range(count)]
    for pivot in range(count):
        for row in range(pivot + 1, count):
            factor = matrix[row][pivot] / matrix[pivot][pivot]
            for col in range(pivot, count):
                matrix[row][col] = matrix[row][col] - factor * matrix[pivot][col]
            vector[row] = vector[row] - factor * vector[pivot]
    result = [None] * count
    for row in range(count - 1, -1, -1):
        total = vector[row]
        for col in range(row + 1, count):
            total = total - matrix[row][col] * result[col]
        result[row] = total / matrix[row][row]
    return result

def reference(rhs, guess, blocks, valve, jscale, prolong, agg_map, cdiag, coff, send_rows, recv_rows, live_counts):

    def apply_a(field):
        return operate(field, blocks, valve, send_rows, recv_rows, live_counts)
    first = rhs - apply_a(guess)
    beta = jnp.sqrt(jnp.sum(first * first))
    basis = [first / beta]
    directions = []
    hess = jnp.zeros((ITERS + 1, ITERS), jnp.float32)
    for column in range(ITERS):
        direction = precondition(basis[column], jscale, prolong, agg_map, cdiag, coff)
        image = apply_a(direction)
        heights = jnp.stack([jnp.sum(vector * image) for vector in basis])
        energy = jnp.sum(image * image)
        for row in range(column + 1):
            image = image - heights[row] * basis[row]
        remainder = energy - jnp.sum(heights * heights)
        height = jnp.sqrt(jnp.maximum(remainder, 0.01 * energy))
        hess = hess.at[:column + 1, column].set(heights).at[column + 1, column].set(height)
        basis.append(image / height)
        directions.append(direction)
    gram = jnp.dot(hess.T, hess, precision=lax.Precision.HIGHEST)
    coeffs = solve_small(gram, beta * hess[0])
    solution = guess
    for column in range(ITERS):
        solution = solution + coeffs[column] * directions[column]
    return (solution, basis[ITERS])
```

```python
import jax
import jax.numpy as jnp
from jax import lax
from jax.experimental import pallas as pl
from jax.experimental.pallas import tpu as pltpu
from jax.sharding import PartitionSpec as P

F32 = jnp.float32
BF16 = jnp.bfloat16
I32 = jnp.int32
MESH = pl.DeviceIdType.MESH

BS, NB, CPD = 64, 128, 48
NY, NZ, NG = 8, 12, 8
NSUB = NY * NZ
PLANE = NY * NG
ROWS = 3 * NY
NC = NSUB * NG * CPD
HALOS = 6
Z_ORDER = (6, 5, 7, 4, 8, 3, 9, 2, 10, 1, 11)


def iota(shape, dim):
    return lax.broadcasted_iota(I32, shape, dim)


def total(x):
    return jnp.sum(jnp.sum(x, axis=0, keepdims=True), axis=1, keepdims=True)


def kernel(
    rhs_h, guess_h, blocks_h, valve_h, jscale_h, prolong_h, agg_h, cdiag_h, coff_h, send_h, recv_h, live_h,
    sol_ref, next_ref,
    rhs, guess, blocks, valve, jscale, prolong, agg, cdiag, coff, recv, live,
    h_guess, h_prolong, h_send, h_e1, h_e2, h_sp1, h_sp2,
    plane1, plane2, plane3, line1, line2, scal1, scal2, scal3,
    onehot, link, xr, cb1, field, out_l, f_b1, f_d1, f_im1, f_b2, f_d2, e1, e2, sp1, sp2,
    load_sem, hs_sem, hr_sem, ps_sem, pr_sem, ls_sem, lr_sem,
):
    s = lax.axis_index("sub")
    g = lax.axis_index("grp")
    y = s // NZ
    z = s % NZ
    me = g * NY + y
    up = {"sub": (s + 1) % NSUB}
    down = {"sub": (s + NSUB - 1) % NSUB}

    def plane_dev(t):
        return {"sub": (t % NY) * NZ + z, "grp": t // NY}

    def line_dev(dz):
        return {"sub": y * NZ + (z + dz) % NZ}

    barrier = pltpu.get_barrier_semaphore()
    for where in (up, down):
        pl.semaphore_signal(barrier, inc=1, device_id=where, device_id_type=MESH)
    for dz in Z_ORDER:
        pl.semaphore_signal(barrier, inc=1, device_id=line_dev(dz), device_id_type=MESH)

    def greet(i, carry):
        pl.semaphore_signal(barrier, inc=1, device_id=plane_dev((me + i) % PLANE), device_id_type=MESH)
        return carry

    lax.fori_loop(1, PLANE, greet, 0)

    loads = [
        pltpu.make_async_copy(src, dst, load_sem.at[i])
        for i, (src, dst) in enumerate(
            (
                (guess_h, guess), (blocks_h, blocks), (rhs_h, rhs), (valve_h, valve), (prolong_h, prolong),
                (agg_h, agg), (recv_h, recv), (live_h, live), (jscale_h, jscale), (cdiag_h, cdiag), (coff_h, coff),
            )
        )
    ]
    for load in loads:
        load.start()

    pl.semaphore_wait(barrier, 2 + len(Z_ORDER) + PLANE - 1)

    def halo(which, src, dst):
        return [
            pltpu.make_async_remote_copy(
                src, dst.at[side], hs_sem.at[which, side], hr_sem.at[which, side],
                device_id=where, device_id_type=MESH,
            )
            for side, where in ((0, up), (1, down))
        ]

    halo_guess = halo(0, guess_h.at[0, 0], h_guess)
    halo_send = halo(1, send_h.at[0, 0], h_send)
    halo_prolong = halo(2, prolong_h.at[0, 0], h_prolong)
    halo_e1 = halo(3, e1, h_e1)
    halo_e2 = halo(4, e2, h_e2)
    halo_sp1 = halo(5, sp1, h_sp1)
    halo_sp2 = halo(6, sp2, h_sp2)
    for copy in halo_guess + halo_send + halo_prolong:
        copy.start()

    def across_plane(buf, which):
        def one(off):
            t = (me + off) % PLANE
            return pltpu.make_async_remote_copy(
                buf.at[pl.ds(me, 1)], buf.at[pl.ds(me, 1)], ps_sem.at[which], pr_sem.at[which],
                device_id=plane_dev(t), device_id_type=MESH,
            )

        def body(i, carry):
            one(i).start()
            return carry

        lax.fori_loop(PLANE // 2 + NY // 2, PLANE, body, 0)
        lax.fori_loop(1, PLANE // 2 + NY // 2, body, 0)

    def plane_all(buf, which):
        return pltpu.make_async_remote_copy(
            buf.at[pl.ds(0, PLANE - 1)], buf.at[pl.ds(0, PLANE - 1)], ps_sem.at[which], pr_sem.at[which],
            device_id=up, device_id_type=MESH,
        )

    def across_line(buf, which):
        for dz in Z_ORDER:
            pltpu.make_async_remote_copy(
                buf.at[z], buf.at[z], ls_sem.at[which], lr_sem.at[which],
                device_id=line_dev(dz), device_id_type=MESH,
            ).start()

    def line_all(buf, which):
        return pltpu.make_async_remote_copy(
            buf.at[pl.ds(0, NZ - 1)], buf.at[pl.ds(0, NZ - 1)], ls_sem.at[which], lr_sem.at[which],
            device_id=up, device_id_type=MESH,
        )

    lane = iota((1, NB), 1)
    spare = (CPD * (g + 1)) % NB

    def apply_local(v):
        def body(t, carry):
            rows = []
            for i in range(8):
                prod = blocks[0, 0, 8 * t + i].astype(F32) * v
                acc = prod[0:8]
                for j in range(1, 8):
                    acc = acc + prod[8 * j : 8 * j + 8]
                rows.append(jnp.sum(acc, axis=0, keepdims=True))
            out_l[pl.ds(pl.multiple_of(8 * t, 8), 8), :] = jnp.concatenate(rows, axis=0)
            return carry

        lax.fori_loop(0, BS // 8, body, 0)
        return out_l[...] + (3.0 * valve[0].astype(F32)) * v

    def apply_link(below, above):
        both = jnp.concatenate([below, above], axis=1)
        hi = both.astype(BF16)
        lo = (both - hi.astype(F32)).astype(BF16)
        out = jnp.dot(jnp.concatenate([hi, lo], axis=0), link[...], preferred_element_type=F32)
        return out[:BS] + out[BS:]

    def restrict(v):
        weighted = jnp.sum(prolong[0, 0] * v, axis=0, keepdims=True)
        return jnp.sum(onehot[...] * weighted, axis=1, keepdims=True)

    def message(column, scalars):
        place = iota((CPD, NB), 1) == (iota((CPD, NB), 0) + CPD * g) % NB
        row = jnp.sum(jnp.where(place, column, 0.0), axis=0, keepdims=True)
        for i, value in enumerate(scalars):
            row = jnp.where(lane == spare + i, value, row)
        return row

    def gather(plane, line, scal, which):
        across_plane(plane, which)
        plane_all(plane, which).wait_recv()
        spot = iota((NY, NB), 1)
        parts = [None] * 3
        extra = None
        for gg in range(NG):
            v = plane[NY * gg : NY * gg + NY, :]
            for k in range(3):
                lo, hi = max(CPD * gg, NB * k), min(CPD * gg + CPD, NB * k + NB)
                if lo < hi:
                    term = jnp.where((spot >= lo - NB * k) & (spot < hi - NB * k), v, 0.0)
                    parts[k] = term if parts[k] is None else parts[k] + term
            at = (CPD * (gg + 1)) % NB
            term = jnp.where((spot == at) | (spot == at + 1), v, 0.0)
            extra = term if extra is None else extra + term
        for k in range(3):
            line[z, NY * k : NY * k + NY, :] = parts[k]
        scal[z] = jnp.sum(extra, axis=0, keepdims=True)
        across_line(scal, which)
        across_line(line, 3 + which)
        line_all(scal, which).wait_recv()
        line_all(line, 3 + which).wait_recv()
        sums = jnp.sum(scal[...], axis=0)
        return [jnp.sum(jnp.where(lane % 16 == i, sums, 0.0), axis=1, keepdims=True) for i in (0, 1)]

    def coarse_product():
        def body(zz, acc):
            for k in range(3):
                for yy in range(NY):
                    at = pl.multiple_of(((yy * NZ + zz) * 3 + k) * NB, NB)
                    r = NY * k + yy
                    acc = acc + coff[:, pl.ds(at, NB)].astype(F32) * xr[zz, r : r + 1, :]
            return acc

        acc = lax.fori_loop(0, NZ, body, jnp.zeros((CPD, NB), F32))
        return jnp.sum(acc, axis=1, keepdims=True)

    def spread_of(column):
        eye = iota((CPD, CPD), 0) == iota((CPD, CPD), 1)
        diag = jnp.sum(jnp.where(eye, cdiag[...].reshape(1, CPD), 0.0), axis=1, keepdims=True)
        sol = diag * column + coarse_product()
        return jnp.sum(onehot[...] * sol, axis=0, keepdims=True)

    loads[0].wait()
    loads[1].wait()
    loads[3].wait()
    field[...] = apply_local(guess[0, 0])
    for i in (2, 4, 5, 6, 7, 8, 9):
        loads[i].wait()
    onehot[...] = jnp.where(iota((CPD, NB), 0) == agg[0], 1.0, 0.0)
    for copy in halo_send:
        copy.wait_recv()
    for side in (0, 1):
        rows_i = iota((NB, NB), 0)
        took = jnp.where(rows_i == h_send[side][side : side + 1, :], 1.0, 0.0).astype(BF16)
        alive = iota((NB, NB), 1) < live[0][:, side : side + 1]
        puts = jnp.where((rows_i == recv[0, 0][side : side + 1, :]) & alive, 1.0, 0.0).astype(BF16)
        both = lax.dot_general(took, puts, (((1,), (1,)), ((), ())), preferred_element_type=F32)
        end = 0 if side == 0 else NSUB - 1
        both = both * jnp.where(s == end, 0.0, -0.5)
        link[NB * side : NB * side + NB, :] = both.astype(BF16)
    for copy in halo_guess:
        copy.wait_recv()
    first = rhs[0, 0] - field[...] - apply_link(h_guess[0], h_guess[1])
    own1 = restrict(first)
    plane1[pl.ds(me, 1), :] = message(own1, [total(first * first), jnp.zeros((1, 1), F32)])
    e1[...] = jscale[0, 0] * first
    for copy in halo_e1:
        copy.start()
    f_b1[...] = first

    square, _ = gather(plane1, line1, scal1, 0)
    beta = jnp.sqrt(square)
    inv1 = 1.0 / beta
    for zz in range(NZ):
        x = line1[zz] * inv1
        cb1[zz] = x
        xr[zz] = x.astype(BF16).astype(F32)
    own1 = own1 * inv1
    loads[10].wait()
    spread = spread_of(own1)
    sp1[...] = spread
    for copy in halo_sp1:
        copy.start()
    f_b1[...] = f_b1[...] * inv1
    f_d1[...] = jscale[0, 0] * f_b1[...] + prolong[0, 0] * spread
    field[...] = apply_local(f_d1[...])
    for copy in halo_prolong + halo_e1 + halo_sp1:
        copy.wait_recv()
    image = field[...] + apply_link(
        *[h_e1[side] * inv1 + h_prolong[side] * h_sp1[side] for side in (0, 1)]
    )
    own2 = restrict(image)
    plane2[pl.ds(me, 1), :] = message(own2, [total(f_b1[...] * image), total(image * image)])
    e2[...] = jscale[0, 0] * image
    for copy in halo_e2:
        copy.start()
    f_im1[...] = image

    h11, energy = gather(plane2, line2, scal2, 1)
    h21 = jnp.sqrt(jnp.maximum(energy - h11 * h11, 0.01 * energy))
    inv2 = 1.0 / h21
    for zz in range(NZ):
        x = (line2[zz] - h11 * cb1[zz]) * inv2
        xr[zz] = x.astype(BF16).astype(F32)
    own2 = (own2 - h11 * own1) * inv2
    spread = spread_of(own2)
    sp2[...] = spread
    for copy in halo_sp2:
        copy.start()
    f_b2[...] = (f_im1[...] - h11 * f_b1[...]) * inv2
    f_d2[...] = jscale[0, 0] * f_b2[...] + prolong[0, 0] * spread
    field[...] = apply_local(f_d2[...])
    for copy in halo_e2 + halo_sp2:
        copy.wait_recv()
    back = h11 * inv1
    image = field[...] + apply_link(
        *[(h_e2[side] - back * h_e1[side]) * inv2 + h_prolong[side] * h_sp2[side] for side in (0, 1)]
    )

    row = jnp.zeros((1, NB), F32)
    for i, value in enumerate((total(f_b1[...] * image), total(f_b2[...] * image), total(image * image))):
        row = jnp.where(lane == i, value, row)
    plane3[pl.ds(me, 1), :] = row
    across_plane(plane3, 2)
    plane_all(plane3, 2).wait_recv()
    scal3[z] = jnp.sum(plane3[...], axis=0, keepdims=True)
    across_line(scal3, 2)
    line_all(scal3, 2).wait_recv()
    sums = jnp.sum(scal3[...], axis=0)
    h12, h22, energy = [jnp.sum(jnp.where(lane == i, sums, 0.0), axis=1, keepdims=True) for i in range(3)]
    h32 = jnp.sqrt(jnp.maximum(energy - (h12 * h12 + h22 * h22), 0.01 * energy))
    g00 = h11 * h11 + h21 * h21
    g01 = h11 * h12 + h21 * h22
    g11 = h12 * h12 + h22 * h22 + h32 * h32
    factor = g01 / g00
    t0 = beta * h11
    t1 = beta * h12 - factor * t0
    c1 = t1 / (g11 - factor * g01)
    c0 = (t0 - g01 * c1) / g00
    next_ref[0, 0] = (image - h12 * f_b1[...] - h22 * f_b2[...]) * (1.0 / h32)
    sol_ref[0, 0] = guess[0, 0] + c0 * f_d1[...] + c1 * f_d2[...]

    for copy in halo_guess + halo_send + halo_prolong + halo_e1 + halo_e2 + halo_sp1 + halo_sp2:
        copy.wait_send()
    for which, buf in enumerate((plane1, plane2, plane3)):
        plane_all(buf, which).wait_send()
    for which, buf in enumerate((scal1, scal2, scal3, line1, line2)):
        line_all(buf, which).wait_send()


def on_device(*args):
    field = (BS, NB)
    hbm_spec = pl.BlockSpec(memory_space=pltpu.HBM)
    vmem_spec = pl.BlockSpec(memory_space=pltpu.VMEM)
    sides = (2, BS, NB)
    shape = jax.ShapeDtypeStruct((1, 1, BS, NB), F32)
    return pl.pallas_call(
        kernel,
        out_shape=(shape, shape),
        in_specs=[hbm_spec] * 12,
        out_specs=(vmem_spec, vmem_spec),
        scratch_shapes=[
            *[pltpu.VMEM(args[i].shape, args[i].dtype) for i in (0, 1, 2, 3, 4, 5, 6, 7, 8, 10, 11)],
            pltpu.VMEM(sides, F32),
            pltpu.VMEM(sides, F32),
            pltpu.VMEM((2, 2, NB), I32),
            pltpu.VMEM(sides, F32),
            pltpu.VMEM(sides, F32),
            pltpu.VMEM((2, 1, NB), F32),
            pltpu.VMEM((2, 1, NB), F32),
            *[pltpu.VMEM((PLANE, NB), F32)] * 3,
            *[pltpu.VMEM((NZ, ROWS, NB), F32)] * 2,
            *[pltpu.VMEM((NZ, 1, NB), F32)] * 3,
            pltpu.VMEM((CPD, NB), F32),
            pltpu.VMEM((2 * NB, NB), BF16),
            pltpu.VMEM((NZ, ROWS, NB), F32),
            pltpu.VMEM((NZ, ROWS, NB), F32),
            *[pltpu.VMEM(field, F32)] * 9,
            pltpu.VMEM((1, NB), F32),
            pltpu.VMEM((1, NB), F32),
            pltpu.SemaphoreType.DMA((11,)),
            pltpu.SemaphoreType.DMA((7, 2)),
            pltpu.SemaphoreType.DMA((7, 2)),
            pltpu.SemaphoreType.DMA((3,)),
            pltpu.SemaphoreType.DMA((3,)),
            pltpu.SemaphoreType.DMA((5,)),
            pltpu.SemaphoreType.DMA((5,)),
        ],
        compiler_params=pltpu.CompilerParams(
            collective_id=0, has_side_effects=True, vmem_limit_bytes=61900 * 1024
        ),
    )(*args)


def solution(mesh):
    return jax.shard_map(
        on_device,
        mesh=mesh,
        in_specs=(
            P("sub", "grp", None, None),
            P("sub", "grp", None, None),
            P("sub", "grp", None, None, None),
            P("sub", "grp", None),
            P("sub", "grp", None, None),
            P("sub", "grp", None, None),
            P("sub", "grp", None),
            P(("sub", "grp")),
            P(("sub", "grp"), None),
            P("sub", "grp", None, None),
            P("sub", "grp", None, None),
            P("sub", "grp", None),
        ),
        out_specs=(P("sub", "grp", None, None), P("sub", "grp", None, None)),
        check_vma=False,
    )
```

```python
import jax
import jax.numpy as jnp
from jax import lax
from jax.experimental import pallas as pl
from jax.experimental.pallas import tpu as pltpu
from jax.sharding import PartitionSpec as P

F32 = jnp.float32
BF16 = jnp.bfloat16
I32 = jnp.int32
MESH = pl.DeviceIdType.MESH

BS, NB, CPD = 64, 128, 48
NY, NZ, NG = 8, 12, 8
NSUB = NY * NZ
PLANE = NY * NG
NC = NSUB * NG * CPD
NEAR = (0, 1, 2, 7)
HALF = 12
Z_ORDER = (6, 5, 7, 4, 8, 3, 9, 2, 10, 1, 11)


def iota(shape, dim):
    return lax.broadcasted_iota(I32, shape, dim)


def total(x):
    return jnp.sum(jnp.sum(x, axis=0, keepdims=True), axis=1, keepdims=True)


def kernel(
    rhs_h, guess_h, blocks_h, valve_h, jscale_h, prolong_h, agg_h, cdiag_h, coff_h, send_h, recv_h, live_h,
    sol_ref, next_ref,
    rhs, guess, blocks, valve, jscale, prolong, agg, cdiag, coff, recv, live,
    h_guess, h_prolong, h_send, h_e1, h_e2, h_sp1, h_sp2,
    plane1, plane2, plane3, line1, line2, scal3,
    onehot, place, diag, link, wide, xs, cs, field, out_l, f_b1, f_d1, f_im1, f_b2, f_d2, e1, e2, sp1, sp2,
    load_sem, hs_sem, hr_sem, ps_sem, pr_sem, ls_sem, lr_sem, fs_sem, fr_sem, cs_sem, cr_sem, sync,
):
    s = lax.axis_index("sub")
    g = lax.axis_index("grp")
    y = s // NZ
    z = s % NZ
    me = g * NY + y
    mine = NY * g + 2
    core = g % 2
    sibling = {"grp": g + 1 - 2 * core}
    up = {"sub": (s + 1) % NSUB}
    down = {"sub": (s + NSUB - 1) % NSUB}

    def plane_dev(t):
        return {"sub": (t % NY) * NZ + z, "grp": t // NY}

    def line_dev(dz):
        return {"sub": y * NZ + (z + dz) % NZ}

    barrier = pltpu.get_barrier_semaphore()

    def greet(where):
        pl.semaphore_signal(barrier, inc=1, device_id=where, device_id_type=MESH)

    for where in (up, down):
        greet({**where, "grp": g + 1 - core})

    @pl.when(core == 0)
    def _():
        greet(sibling)

    def greet_plane(t, carry):
        greet({"sub": ((y + t // 4) % NY) * NZ + z, "grp": ((g // 2 + t) % 4) * 2})
        return carry

    def greet_line(i, carry):
        greet({"sub": y * NZ + (z + i) % NZ, "grp": g - core})
        return carry

    lax.fori_loop(16, 32, greet_plane, 0)
    lax.fori_loop(1, NZ, greet_line, 0)
    lax.fori_loop(1, 16, greet_plane, 0)

    @pl.when(core == 1)
    def _():
        greet(sibling)

    loads = [
        pltpu.make_async_copy(src, dst, load_sem.at[i])
        for i, (src, dst) in enumerate(
            (
                (guess_h, guess), (blocks_h, blocks), (rhs_h, rhs), (valve_h, valve), (prolong_h, prolong),
                (agg_h, agg), (recv_h, recv), (live_h, live), (jscale_h, jscale), (cdiag_h, cdiag), (coff_h, coff),
            )
        )
    ]
    for load in loads:
        load.start()

    loads[0].wait()
    loads[4].wait()

    @pl.when(core == 1)
    def _():
        pl.semaphore_wait(barrier, 5)
        pl.semaphore_signal(sync, inc=1, device_id=sibling, device_id_type=MESH)

    @pl.when(core == 0)
    def _():
        pl.semaphore_wait(sync, 1)

    def halo(which, src, dst):
        return [
            pltpu.make_async_remote_copy(
                src, dst.at[side], hs_sem.at[which, side], hr_sem.at[which, side],
                device_id=where, device_id_type=MESH,
            )
            for side, where in ((0, up), (1, down))
        ]

    halo_guess = halo(0, guess.at[0, 0], h_guess)
    halo_send = halo(1, send_h.at[0, 0], h_send)
    halo_prolong = halo(2, prolong.at[0, 0], h_prolong)
    halo_e1 = halo(3, e1, h_e1)
    halo_e2 = halo(4, e2, h_e2)
    halo_sp1 = halo(5, sp1, h_sp1)
    halo_sp2 = halo(6, sp2, h_sp2)
    for copy in halo_guess + halo_send + halo_prolong:
        copy.start()

    def across_plane(buf, which):
        for oy in (4, 3, 5, 2, 6, 1, 7, 0):
            cls = 0 if oy in NEAR else 1

            def one(i, carry):
                pltpu.make_async_remote_copy(
                    buf.at[pl.ds(mine, 1)], buf.at[pl.ds(NY * g + (2 - oy) % NY, 1)],
                    ps_sem.at[which, cls], pr_sem.at[which, cls],
                    device_id={"sub": ((y + oy) % NY) * NZ + z, "grp": (g + i) % NG}, device_id_type=MESH,
                ).start()
                return carry

            lax.fori_loop(4, NG, one, 0)
            lax.fori_loop(0 if oy else 1, 4, one, 0)

    def plane_all(buf, which, cls):
        count = NG * 4 - 1 if cls == 0 else NG * 4
        return pltpu.make_async_remote_copy(
            buf.at[pl.ds(0, count)], buf.at[pl.ds(0, count)], ps_sem.at[which, cls], pr_sem.at[which, cls],
            device_id=up, device_id_type=MESH,
        )

    def line_copy(buf, dz, which):
        return pltpu.make_async_remote_copy(
            buf.at[core, z], buf.at[core, z], ls_sem.at[which, dz], lr_sem.at[which, dz],
            device_id=line_dev(dz), device_id_type=MESH,
        )

    def hand_over(buf, dz, which):
        at = (z + NZ - dz) % NZ
        return pltpu.make_async_remote_copy(
            buf.at[core, at], buf.at[core, at], fs_sem.at[which], fr_sem.at[which],
            device_id=sibling, device_id_type=MESH,
        )

    def handed_over(buf, which):
        return pltpu.make_async_remote_copy(
            buf.at[0, pl.ds(0, NZ - 1)], buf.at[0, pl.ds(0, NZ - 1)], fs_sem.at[which], fr_sem.at[which],
            device_id=sibling, device_id_type=MESH,
        )

    def scal_copy(dz):
        return pltpu.make_async_remote_copy(
            scal3.at[z], scal3.at[z], cs_sem, cr_sem, device_id=line_dev(dz), device_id_type=MESH,
        )

    scal_all = pltpu.make_async_remote_copy(
        scal3.at[pl.ds(0, NZ - 1)], scal3.at[pl.ds(0, NZ - 1)], cs_sem, cr_sem, device_id=up, device_id_type=MESH,
    )

    lane = iota((1, NB), 1)
    spare = (CPD * (g + 1)) & (NB - 1)

    def apply_local(v):
        def body(t, carry):
            rows = []
            for i in range(8):
                prod = blocks[0, 0, 8 * t + i].astype(F32) * v
                acc = prod[0:8]
                for j in range(1, 8):
                    acc = acc + prod[8 * j : 8 * j + 8]
                rows.append(jnp.sum(acc, axis=0, keepdims=True))
            out_l[pl.ds(pl.multiple_of(8 * t, 8), 8), :] = jnp.concatenate(rows, axis=0)
            return carry

        lax.fori_loop(0, BS // 8, body, 0)
        return out_l[...] + (3.0 * valve[0].astype(F32)) * v

    def apply_link(below, above):
        both = jnp.concatenate([below, above], axis=1)
        hi = both.astype(BF16)
        lo = (both - hi.astype(F32)).astype(BF16)
        out = jnp.dot(jnp.concatenate([hi, lo], axis=0), link[...], preferred_element_type=F32)
        return out[:BS] + out[BS:]

    def restrict(v):
        weighted = jnp.sum(prolong[0, 0] * v, axis=0, keepdims=True)
        return jnp.sum(onehot[...] * weighted, axis=1, keepdims=True)

    def message(column, scalars):
        row = jnp.sum(place[...] * column, axis=0, keepdims=True)
        for i, value in enumerate(scalars):
            row = jnp.where(lane == spare + i, value, row)
        return row

    def pick(plane, first_row, count):
        spot = iota((count, NB), 1)
        parts = [None] * 3
        extra = None
        for gg in range(NG):
            v = plane[NY * gg + first_row : NY * gg + first_row + count, :]
            for k in range(3):
                lo, hi = max(CPD * gg, NB * k), min(CPD * gg + CPD, NB * k + NB)
                if lo < hi:
                    term = jnp.where((spot >= lo - NB * k) & (spot < hi - NB * k), v, 0.0)
                    parts[k] = term if parts[k] is None else parts[k] + term
            at = (CPD * (gg + 1)) % NB
            term = jnp.where((spot == at) | (spot == at + 1), v, 0.0)
            extra = term if extra is None else extra + term
        return parts, jnp.sum(extra, axis=0, keepdims=True)

    def gather(plane, line, which):
        def send_own():
            for dz in Z_ORDER:
                line_copy(line, dz, which).start()

        plane_all(plane, which, 0).wait_recv()
        parts, some = pick(plane, 0, 4)
        for k in range(3):
            line[0, z, 4 * k : 4 * k + 4, :] = parts[k]
        line[0, z, HALF : HALF + 1, :] = jnp.zeros((1, NB), F32)
        pl.when(core == 0)(send_own)
        plane_all(plane, which, 1).wait_recv()
        parts, rest = pick(plane, 4, 4)
        for k in range(3):
            line[1, z, 4 * k : 4 * k + 4, :] = parts[k]
        line[1, z, HALF : HALF + 1, :] = some + rest
        pl.when(core == 1)(send_own)
        for dz in reversed(Z_ORDER):
            line_copy(line, dz, which).wait_recv()
            hand_over(line, dz, which).start()
        handed_over(line, which).wait_recv()
        sums = jnp.sum(line[1, :, HALF, :], axis=0, keepdims=True)
        return [jnp.sum(jnp.where(lane & 15 == i, sums, 0.0), axis=1, keepdims=True) for i in (0, 1)]

    def coarse_product():
        def body(zz, acc):
            for r in range(NY):
                base = (((y + r + NY - 2) % NY) * NZ + zz) * 3
                for k in range(3):
                    at = pl.multiple_of((base + k) * NB, NB)
                    row = 4 * k + r % 4
                    acc = acc + wide[:, pl.ds(at, NB)] * xs[r // 4, zz, row : row + 1, :]
            return acc

        acc = lax.fori_loop(0, NZ, body, jnp.zeros((CPD, NB), F32))
        return jnp.sum(acc, axis=1, keepdims=True)

    def spread_of(column):
        sol = diag[:, 0:1] * column + coarse_product()
        return jnp.sum(onehot[...] * sol, axis=0, keepdims=True)

    loads[1].wait()
    loads[3].wait()
    field[...] = apply_local(guess[0, 0])
    for i in (2, 5, 6, 7, 8, 9):
        loads[i].wait()
    onehot[...] = jnp.where(iota((CPD, NB), 0) == agg[0], 1.0, 0.0)
    place[...] = jnp.where(iota((CPD, NB), 1) == (iota((CPD, NB), 0) + CPD * g) & (NB - 1), 1.0, 0.0)
    eye = iota((CPD, CPD), 0) == iota((CPD, CPD), 1)
    diag[...] = jnp.zeros((CPD, NB), F32) + jnp.sum(
        jnp.where(eye, cdiag[...].reshape(1, CPD), 0.0), axis=1, keepdims=True
    )
    for copy in halo_send:
        copy.wait_recv()
    for side in (0, 1):
        rows_i = iota((NB, NB), 0)
        took = jnp.where(rows_i == h_send[side][side : side + 1, :], 1.0, 0.0).astype(BF16)
        alive = iota((NB, NB), 1) < live[0][:, side : side + 1]
        puts = jnp.where((rows_i == recv[0, 0][side : side + 1, :]) & alive, 1.0, 0.0).astype(BF16)
        both = lax.dot_general(took, puts, (((1,), (1,)), ((), ())), preferred_element_type=F32)
        end = 0 if side == 0 else NSUB - 1
        both = both * jnp.where(s == end, 0.0, -0.5)
        link[NB * side : NB * side + NB, :] = both.astype(BF16)

    @pl.when(core == 0)
    def _():
        pl.semaphore_wait(barrier, PLANE - 1 + 2 * (NZ - 1))
        pl.semaphore_signal(sync, inc=1, device_id=sibling, device_id_type=MESH)

    for copy in halo_guess:
        copy.wait_recv()
    first = rhs[0, 0] - field[...] - apply_link(h_guess[0], h_guess[1])
    own1 = restrict(first)
    plane1[pl.ds(mine, 1), :] = message(own1, [total(first * first), jnp.zeros((1, 1), F32)])

    @pl.when(core == 1)
    def _():
        pl.semaphore_wait(sync, 1)

    across_plane(plane1, 0)
    e1[...] = jscale[0, 0] * first
    for copy in halo_e1:
        copy.start()
    f_b1[...] = first
    loads[10].wait()

    def widen(i, carry):
        at = pl.multiple_of(i * 8 * NB, NB)
        wide[:, pl.ds(at, 8 * NB)] = coff[:, pl.ds(at, 8 * NB)].astype(F32)
        return carry

    lax.fori_loop(0, NC // (8 * NB), widen, 0)

    square, _ = gather(plane1, line1, 0)
    beta = jnp.sqrt(square)
    inv1 = 1.0 / beta
    for zz in range(NZ):
        for half in (0, 1):
            x = line1[half, zz, 0:HALF, :] * inv1
            cs[half, zz] = x
            xs[half, zz] = x.astype(BF16).astype(F32)
    own1 = own1 * inv1
    spread = spread_of(own1)
    sp1[...] = spread
    for copy in halo_sp1:
        copy.start()
    f_b1[...] = f_b1[...] * inv1
    f_d1[...] = jscale[0, 0] * f_b1[...] + prolong[0, 0] * spread
    field[...] = apply_local(f_d1[...])
    for copy in halo_prolong + halo_e1 + halo_sp1:
        copy.wait_recv()
    image = field[...] + apply_link(
        *[h_e1[side] * inv1 + h_prolong[side] * h_sp1[side] for side in (0, 1)]
    )
    own2 = restrict(image)
    plane2[pl.ds(mine, 1), :] = message(own2, [total(f_b1[...] * image), total(image * image)])
    across_plane(plane2, 1)
    e2[...] = jscale[0, 0] * image
    for copy in halo_e2:
        copy.start()
    f_im1[...] = image

    h11, energy = gather(plane2, line2, 1)
    h21 = jnp.sqrt(jnp.maximum(energy - h11 * h11, 0.01 * energy))
    inv2 = 1.0 / h21
    for zz in range(NZ):
        for half in (0, 1):
            x = (line2[half, zz, 0:HALF, :] - h11 * cs[half, zz]) * inv2
            xs[half, zz] = x.astype(BF16).astype(F32)
    own2 = (own2 - h11 * own1) * inv2
    spread = spread_of(own2)
    sp2[...] = spread
    for copy in halo_sp2:
        copy.start()
    f_b2[...] = (f_im1[...] - h11 * f_b1[...]) * inv2
    f_d2[...] = jscale[0, 0] * f_b2[...] + prolong[0, 0] * spread
    field[...] = apply_local(f_d2[...])
    for copy in halo_e2 + halo_sp2:
        copy.wait_recv()
    back = h11 * inv1
    image = field[...] + apply_link(
        *[(h_e2[side] - back * h_e1[side]) * inv2 + h_prolong[side] * h_sp2[side] for side in (0, 1)]
    )

    row = jnp.zeros((1, NB), F32)
    for i, value in enumerate((total(f_b1[...] * image), total(f_b2[...] * image), total(image * image))):
        row = jnp.where(lane == i, value, row)
    plane3[pl.ds(mine, 1), :] = row
    across_plane(plane3, 2)
    g00 = h11 * h11 + h21 * h21
    inv00 = 1.0 / g00
    t0 = beta * h11
    plane_all(plane3, 2, 0).wait_recv()
    plane_all(plane3, 2, 1).wait_recv()
    scal3[z] = jnp.sum(plane3[...], axis=0, keepdims=True)
    for dz in Z_ORDER:
        scal_copy(dz).start()
    scal_all.wait_recv()
    sums = jnp.sum(scal3[...], axis=0)
    h12, h22, energy = [jnp.sum(jnp.where(lane == i, sums, 0.0), axis=1, keepdims=True) for i in range(3)]
    h32 = jnp.sqrt(jnp.maximum(energy - (h12 * h12 + h22 * h22), 0.01 * energy))
    g01 = h11 * h12 + h21 * h22
    g11 = h12 * h12 + h22 * h22 + h32 * h32
    factor = g01 * inv00
    t1 = beta * h12 - factor * t0
    c1 = t1 / (g11 - factor * g01)
    c0 = (t0 - g01 * c1) * inv00
    next_ref[0, 0] = (image - h12 * f_b1[...] - h22 * f_b2[...]) * (1.0 / h32)
    sol_ref[0, 0] = guess[0, 0] + c0 * f_d1[...] + c1 * f_d2[...]

    for copy in halo_guess + halo_send + halo_prolong + halo_e1 + halo_e2 + halo_sp1 + halo_sp2:
        copy.wait_send()
    for which, buf in enumerate((plane1, plane2, plane3)):
        for cls in (0, 1):
            plane_all(buf, which, cls).wait_send()
    for which, buf in enumerate((line1, line2)):
        for dz in Z_ORDER:
            line_copy(buf, dz, which).wait_send()
        handed_over(buf, which).wait_send()
    scal_all.wait_send()


def on_device(*args):
    field = (BS, NB)
    hbm_spec = pl.BlockSpec(memory_space=pltpu.HBM)
    vmem_spec = pl.BlockSpec(memory_space=pltpu.VMEM)
    sides = (2, BS, NB)
    shape = jax.ShapeDtypeStruct((1, 1, BS, NB), F32)
    return pl.pallas_call(
        kernel,
        out_shape=(shape, shape),
        in_specs=[hbm_spec] * 12,
        out_specs=(vmem_spec, vmem_spec),
        scratch_shapes=[
            *[pltpu.VMEM(args[i].shape, args[i].dtype) for i in (0, 1, 2, 3, 4, 5, 6, 7, 8, 10, 11)],
            pltpu.VMEM(sides, F32),
            pltpu.VMEM(sides, F32),
            pltpu.VMEM((2, 2, NB), I32),
            pltpu.VMEM(sides, F32),
            pltpu.VMEM(sides, F32),
            pltpu.VMEM((2, 1, NB), F32),
            pltpu.VMEM((2, 1, NB), F32),
            *[pltpu.VMEM((PLANE, NB), F32)] * 3,
            *[pltpu.VMEM((2, NZ, HALF + 1, NB), F32)] * 2,
            pltpu.VMEM((NZ, 1, NB), F32),
            *[pltpu.VMEM((CPD, NB), F32)] * 3,
            pltpu.VMEM((2 * NB, NB), BF16),
            pltpu.VMEM((CPD, NC), F32),
            *[pltpu.VMEM((2, NZ, HALF, NB), F32)] * 2,
            *[pltpu.VMEM(field, F32)] * 9,
            pltpu.VMEM((1, NB), F32),
            pltpu.VMEM((1, NB), F32),
            pltpu.SemaphoreType.DMA((11,)),
            pltpu.SemaphoreType.DMA((7, 2)),
            pltpu.SemaphoreType.DMA((7, 2)),
            pltpu.SemaphoreType.DMA((3, 2)),
            pltpu.SemaphoreType.DMA((3, 2)),
            pltpu.SemaphoreType.DMA((2, NZ)),
            pltpu.SemaphoreType.DMA((2, NZ)),
            pltpu.SemaphoreType.DMA((2,)),
            pltpu.SemaphoreType.DMA((2,)),
            pltpu.SemaphoreType.DMA,
            pltpu.SemaphoreType.DMA,
            pltpu.SemaphoreType.REGULAR,
        ],
        compiler_params=pltpu.CompilerParams(
            collective_id=0, has_side_effects=True, vmem_limit_bytes=40 * 1024 * 1024
        ),
    )(*[pltpu.with_memory_space_constraint(a, pltpu.HBM) for a in args])


def solution(mesh):
    return jax.shard_map(
        on_device,
        mesh=mesh,
        in_specs=(
            P("sub", "grp", None, None),
            P("sub", "grp", None, None),
            P("sub", "grp", None, None, None),
            P("sub", "grp", None),
            P("sub", "grp", None, None),
            P("sub", "grp", None, None),
            P("sub", "grp", None),
            P(("sub", "grp")),
            P(("sub", "grp"), None),
            P("sub", "grp", None, None),
            P("sub", "grp", None, None),
            P("sub", "grp", None),
        ),
        out_specs=(P("sub", "grp", None, None), P("sub", "grp", None, None)),
        check_vma=False,
    )
```

```python
import jax
import jax.numpy as jnp
from jax import lax
from jax.experimental import pallas as pl
from jax.experimental.pallas import tpu as pltpu
from jax.sharding import PartitionSpec as P

F32 = jnp.float32
BF16 = jnp.bfloat16
I32 = jnp.int32
MESH = pl.DeviceIdType.MESH

BS, NB, CPD = 64, 128, 48
NY, NZ, NG = 8, 12, 8
NSUB = NY * NZ
PLANE = NY * NG
NC = NSUB * NG * CPD
NEAR = (0, 1, 2, 7)
HALF = 12
REACH = {6: 3, 5: 4, 4: 5}


def hops(n, size):
    n %= size
    return min(n, size - n)


CHIPS = sorted(((ox, oy) for ox in range(4) for oy in range(NY)), key=lambda o: hops(o[0], 4) + hops(o[1], NY))
COUNTS = [20, 7, 4, 1]
DIRECT = sorted(
    (
        (hops(ox, 4) + hops(oy, NY) + hops(oz, NZ), ox, oy, oz)
        for ox, oy in CHIPS
        for oz in range(NZ)
        if hops(ox, 4) + hops(oy, NY) > REACH.get(hops(oz, NZ), 6)
    ),
    reverse=True,
)
Z_ORDER = (6, 5, 7, 4, 8, 3, 9, 2, 10, 1, 11)


def iota(shape, dim):
    return lax.broadcasted_iota(I32, shape, dim)


def total(x):
    return jnp.sum(jnp.sum(x, axis=0, keepdims=True), axis=1, keepdims=True)


def kernel(
    rhs_h, guess_h, blocks_h, valve_h, jscale_h, prolong_h, agg_h, cdiag_h, coff_h, send_h, recv_h, live_h,
    sol_ref, next_ref,
    rhs, guess, blocks, valve, jscale, prolong, agg, cdiag, coff, recv, live,
    h_guess, h_prolong, h_send, h_e1, h_e2, h_sp1, h_sp2,
    plane1, plane2, plane3, direct, part3, line1, line2, scal3,
    onehot, place, diag, link, wide, xs, cs, field, out_l, f_b1, f_d1, f_im1, f_b2, f_d2, e1, e2, sp1, sp2,
    load_sem, hs_sem, hr_sem, ps_sem, pr_sem, ls_sem, lr_sem, fs_sem, fr_sem, cs_sem, cr_sem, ds_sem, dr_sem, sync,
):
    s = lax.axis_index("sub")
    g = lax.axis_index("grp")
    y = s // NZ
    z = s % NZ
    me = g * NY + y
    mine = NY * g + 2
    core = g % 2
    sibling = {"grp": g + 1 - 2 * core}
    up = {"sub": (s + 1) % NSUB}
    down = {"sub": (s + NSUB - 1) % NSUB}

    def plane_dev(t):
        return {"sub": (t % NY) * NZ + z, "grp": t // NY}

    def line_dev(dz):
        return {"sub": y * NZ + (z + dz) % NZ}

    barrier = pltpu.get_barrier_semaphore()

    def greet(where):
        pl.semaphore_signal(barrier, inc=1, device_id=where, device_id_type=MESH)

    for where in (up, down):
        greet({**where, "grp": g + 1 - core})

    @pl.when(core == 0)
    def _():
        greet(sibling)

    def greet_plane(t, carry):
        greet({"sub": ((y + t // 4) % NY) * NZ + z, "grp": ((g // 2 + t) % 4) * 2})
        return carry

    def greet_line(i, carry):
        greet({"sub": y * NZ + (z + i) % NZ, "grp": g - core})
        return carry

    lax.fori_loop(16, 32, greet_plane, 0)
    lax.fori_loop(1, NZ, greet_line, 0)
    lax.fori_loop(1, 16, greet_plane, 0)

    @pl.when(core == 1)
    def _():
        greet(sibling)

    loads = [
        pltpu.make_async_copy(src, dst, load_sem.at[i])
        for i, (src, dst) in enumerate(
            (
                (guess_h, guess), (blocks_h, blocks), (rhs_h, rhs), (valve_h, valve), (prolong_h, prolong),
                (agg_h, agg), (recv_h, recv), (live_h, live), (jscale_h, jscale), (cdiag_h, cdiag), (coff_h, coff),
            )
        )
    ]
    for load in loads:
        load.start()

    loads[0].wait()
    loads[4].wait()

    @pl.when(core == 1)
    def _():
        pl.semaphore_wait(barrier, 5)
        pl.semaphore_signal(sync, inc=1, device_id=sibling, device_id_type=MESH)

    @pl.when(core == 0)
    def _():
        pl.semaphore_wait(sync, 1)

    def halo(which, src, dst):
        return [
            pltpu.make_async_remote_copy(
                src, dst.at[side], hs_sem.at[which, side], hr_sem.at[which, side],
                device_id=where, device_id_type=MESH,
            )
            for side, where in ((0, up), (1, down))
        ]

    halo_guess = halo(0, guess.at[0, 0], h_guess)
    halo_send = halo(1, send_h.at[0, 0], h_send)
    halo_prolong = halo(2, prolong.at[0, 0], h_prolong)
    halo_e1 = halo(3, e1, h_e1)
    halo_e2 = halo(4, e2, h_e2)
    halo_sp1 = halo(5, sp1, h_sp1)
    halo_sp2 = halo(6, sp2, h_sp2)
    for copy in halo_guess + halo_send + halo_prolong:
        copy.start()

    def across_plane(buf, which):
        for oy in (4, 3, 5, 2, 6, 1, 7, 0):
            cls = 0 if oy in NEAR else 1

            def one(i, carry):
                pltpu.make_async_remote_copy(
                    buf.at[pl.ds(mine, 1)], buf.at[pl.ds(NY * g + (2 - oy) % NY, 1)],
                    ps_sem.at[which, cls], pr_sem.at[which, cls],
                    device_id={"sub": ((y + oy) % NY) * NZ + z, "grp": (g + i) % NG}, device_id_type=MESH,
                ).start()
                return carry

            lax.fori_loop(4, NG, one, 0)
            lax.fori_loop(0 if oy else 1, 4, one, 0)

    def plane_all(buf, which, cls):
        count = NG * 4 - 1 if cls == 0 else NG * 4
        return pltpu.make_async_remote_copy(
            buf.at[pl.ds(0, count)], buf.at[pl.ds(0, count)], ps_sem.at[which, cls], pr_sem.at[which, cls],
            device_id=up, device_id_type=MESH,
        )

    def line_copy(buf, dz, which):
        return pltpu.make_async_remote_copy(
            buf.at[core, z], buf.at[core, z], ls_sem.at[which, dz], lr_sem.at[which, dz],
            device_id=line_dev(dz), device_id_type=MESH,
        )

    def hand_over(buf, dz, which):
        at = (z + NZ - dz) % NZ
        return pltpu.make_async_remote_copy(
            buf.at[core, at], buf.at[core, at], fs_sem.at[which], fr_sem.at[which],
            device_id=sibling, device_id_type=MESH,
        )

    def handed_over(buf, which):
        return pltpu.make_async_remote_copy(
            buf.at[0, pl.ds(0, NZ - 1)], buf.at[0, pl.ds(0, NZ - 1)], fs_sem.at[which], fr_sem.at[which],
            device_id=sibling, device_id_type=MESH,
        )

    def scal_copy(dz):
        cls = max(6 - hops(dz, NZ), 0)
        return pltpu.make_async_remote_copy(
            part3.at[min(cls, 3)], scal3.at[z], cs_sem, cr_sem, device_id=line_dev(dz), device_id_type=MESH,
        )

    def send_direct(first, last):
        for at in range(first, last):
            _, ox, oy, oz = DIRECT[at]
            for flip in (0, 1):
                pltpu.make_async_remote_copy(
                    part3.at[4], direct.at[2 * at + core], ds_sem, dr_sem,
                    device_id={
                        "sub": ((y + oy) % NY) * NZ + (z + oz) % NZ,
                        "grp": ((g // 2 + ox) % 4) * 2 + (core + flip) % 2,
                    },
                    device_id_type=MESH,
                ).start()

    def send_plane3():
        for at in reversed(range(PLANE // 2)):
            ox, oy = CHIPS[at]
            cls = sum(at >= sum(COUNTS[: i + 1]) for i in range(3))
            for flip in (0, 1):
                if at or flip:
                    pltpu.make_async_remote_copy(
                        part3.at[4], plane3.at[2 * at + core], ps_sem.at[2, cls], pr_sem.at[2, cls],
                        device_id={
                            "sub": ((y + oy) % NY) * NZ + z,
                            "grp": ((g // 2 + ox) % 4) * 2 + (core + flip) % 2,
                        },
                        device_id_type=MESH,
                    ).start()

    def plane3_all(cls):
        count = 2 * COUNTS[cls] - (cls == 0)
        return pltpu.make_async_remote_copy(
            plane3.at[pl.ds(0, count)], plane3.at[pl.ds(0, count)], ps_sem.at[2, cls], pr_sem.at[2, cls],
            device_id=up, device_id_type=MESH,
        )

    direct_all = pltpu.make_async_remote_copy(
        direct, direct, ds_sem, dr_sem, device_id=up, device_id_type=MESH,
    )

    scal_all = pltpu.make_async_remote_copy(
        scal3.at[pl.ds(0, NZ - 1)], scal3.at[pl.ds(0, NZ - 1)], cs_sem, cr_sem, device_id=up, device_id_type=MESH,
    )

    lane = iota((1, NB), 1)
    spare = (CPD * (g + 1)) & (NB - 1)

    def apply_local(v):
        def body(t, carry):
            rows = []
            for i in range(8):
                prod = blocks[0, 0, 8 * t + i].astype(F32) * v
                acc = prod[0:8]
                for j in range(1, 8):
                    acc = acc + prod[8 * j : 8 * j + 8]
                rows.append(jnp.sum(acc, axis=0, keepdims=True))
            out_l[pl.ds(pl.multiple_of(8 * t, 8), 8), :] = jnp.concatenate(rows, axis=0)
            return carry

        lax.fori_loop(0, BS // 8, body, 0)
        return out_l[...] + (3.0 * valve[0].astype(F32)) * v

    def apply_link(below, above):
        both = jnp.concatenate([below, above], axis=1)
        hi = both.astype(BF16)
        lo = (both - hi.astype(F32)).astype(BF16)
        out = jnp.dot(jnp.concatenate([hi, lo], axis=0), link[...], preferred_element_type=F32)
        return out[:BS] + out[BS:]

    def restrict(v):
        weighted = jnp.sum(prolong[0, 0] * v, axis=0, keepdims=True)
        return jnp.sum(onehot[...] * weighted, axis=1, keepdims=True)

    def message(column, scalars):
        row = jnp.sum(place[...] * column, axis=0, keepdims=True)
        for i, value in enumerate(scalars):
            row = jnp.where(lane == spare + i, value, row)
        return row

    def pick(plane, first_row, count):
        spot = iota((count, NB), 1)
        parts = [None] * 3
        extra = None
        for gg in range(NG):
            v = plane[NY * gg + first_row : NY * gg + first_row + count, :]
            for k in range(3):
                lo, hi = max(CPD * gg, NB * k), min(CPD * gg + CPD, NB * k + NB)
                if lo < hi:
                    term = jnp.where((spot >= lo - NB * k) & (spot < hi - NB * k), v, 0.0)
                    parts[k] = term if parts[k] is None else parts[k] + term
            at = (CPD * (gg + 1)) % NB
            term = jnp.where((spot == at) | (spot == at + 1), v, 0.0)
            extra = term if extra is None else extra + term
        return parts, jnp.sum(extra, axis=0, keepdims=True)

    def gather(plane, line, which):
        def send_own():
            for dz in Z_ORDER:
                line_copy(line, dz, which).start()

        plane_all(plane, which, 0).wait_recv()
        parts, some = pick(plane, 0, 4)
        for k in range(3):
            line[0, z, 4 * k : 4 * k + 4, :] = parts[k]
        line[0, z, HALF : HALF + 1, :] = jnp.zeros((1, NB), F32)
        pl.when(core == 0)(send_own)
        plane_all(plane, which, 1).wait_recv()
        parts, rest = pick(plane, 4, 4)
        for k in range(3):
            line[1, z, 4 * k : 4 * k + 4, :] = parts[k]
        line[1, z, HALF : HALF + 1, :] = some + rest
        pl.when(core == 1)(send_own)
        for dz in reversed(Z_ORDER):
            line_copy(line, dz, which).wait_recv()
            hand_over(line, dz, which).start()
        handed_over(line, which).wait_recv()
        sums = jnp.sum(line[1, :, HALF, :], axis=0, keepdims=True)
        return [jnp.sum(jnp.where(lane & 15 == i, sums, 0.0), axis=1, keepdims=True) for i in (0, 1)]

    def coarse_product():
        def body(zz, acc):
            for r in range(NY):
                base = (((y + r + NY - 2) % NY) * NZ + zz) * 3
                for k in range(3):
                    row = 4 * k + r % 4
                    acc = acc + wide[base + k] * xs[r // 4, zz, row : row + 1, :]
            return acc

        acc = lax.fori_loop(0, NZ, body, jnp.zeros((CPD, NB), F32))
        return jnp.sum(acc, axis=1, keepdims=True)

    def spread_of(column):
        sol = diag[:, 0:1] * column + coarse_product()
        return jnp.sum(onehot[...] * sol, axis=0, keepdims=True)

    loads[1].wait()
    loads[3].wait()
    field[...] = apply_local(guess[0, 0])
    for i in (2, 5, 6, 7, 8, 9):
        loads[i].wait()
    onehot[...] = jnp.where(iota((CPD, NB), 0) == agg[0], 1.0, 0.0)
    place[...] = jnp.where(iota((CPD, NB), 1) == (iota((CPD, NB), 0) + CPD * g) & (NB - 1), 1.0, 0.0)
    eye = iota((CPD, CPD), 0) == iota((CPD, CPD), 1)
    diag[...] = jnp.zeros((CPD, NB), F32) + jnp.sum(
        jnp.where(eye, cdiag[...].reshape(1, CPD), 0.0), axis=1, keepdims=True
    )
    for copy in halo_send:
        copy.wait_recv()
    for side in (0, 1):
        rows_i = iota((NB, NB), 0)
        took = jnp.where(rows_i == h_send[side][side : side + 1, :], 1.0, 0.0).astype(BF16)
        alive = iota((NB, NB), 1) < live[0][:, side : side + 1]
        puts = jnp.where((rows_i == recv[0, 0][side : side + 1, :]) & alive, 1.0, 0.0).astype(BF16)
        both = lax.dot_general(took, puts, (((1,), (1,)), ((), ())), preferred_element_type=F32)
        end = 0 if side == 0 else NSUB - 1
        both = both * jnp.where(s == end, 0.0, -0.5)
        link[NB * side : NB * side + NB, :] = both.astype(BF16)

    @pl.when(core == 0)
    def _():
        pl.semaphore_wait(barrier, PLANE - 1 + 2 * (NZ - 1))
        pl.semaphore_signal(sync, inc=1, device_id=sibling, device_id_type=MESH)

    for copy in halo_guess:
        copy.wait_recv()
    first = rhs[0, 0] - field[...] - apply_link(h_guess[0], h_guess[1])
    own1 = restrict(first)
    plane1[pl.ds(mine, 1), :] = message(own1, [total(first * first), jnp.zeros((1, 1), F32)])

    @pl.when(core == 1)
    def _():
        pl.semaphore_wait(sync, 1)

    across_plane(plane1, 0)
    e1[...] = jscale[0, 0] * first
    for copy in halo_e1:
        copy.start()
    f_b1[...] = first
    loads[10].wait()

    def widen(i, carry):
        for j in range(8):
            at = pl.multiple_of((i * 8 + j) * NB, NB)
            wide[i * 8 + j] = coff[:, pl.ds(at, NB)].astype(F32)
        return carry

    lax.fori_loop(0, NC // (8 * NB), widen, 0)

    square, _ = gather(plane1, line1, 0)
    beta = jnp.sqrt(square)
    inv1 = 1.0 / beta
    for zz in range(NZ):
        for half in (0, 1):
            x = line1[half, zz, 0:HALF, :] * inv1
            cs[half, zz] = x
            xs[half, zz] = x.astype(BF16).astype(F32)
    own1 = own1 * inv1
    spread = spread_of(own1)
    sp1[...] = spread
    for copy in halo_sp1:
        copy.start()
    f_b1[...] = f_b1[...] * inv1
    f_d1[...] = jscale[0, 0] * f_b1[...] + prolong[0, 0] * spread
    field[...] = apply_local(f_d1[...])
    for copy in halo_prolong + halo_e1 + halo_sp1:
        copy.wait_recv()
    image = field[...] + apply_link(
        *[h_e1[side] * inv1 + h_prolong[side] * h_sp1[side] for side in (0, 1)]
    )
    own2 = restrict(image)
    plane2[pl.ds(mine, 1), :] = message(own2, [total(f_b1[...] * image), total(image * image)])
    across_plane(plane2, 1)
    e2[...] = jscale[0, 0] * image
    for copy in halo_e2:
        copy.start()
    f_im1[...] = image

    h11, energy = gather(plane2, line2, 1)
    h21 = jnp.sqrt(jnp.maximum(energy - h11 * h11, 0.01 * energy))
    inv2 = 1.0 / h21
    for zz in range(NZ):
        for half in (0, 1):
            x = (line2[half, zz, 0:HALF, :] - h11 * cs[half, zz]) * inv2
            xs[half, zz] = x.astype(BF16).astype(F32)
    own2 = (own2 - h11 * own1) * inv2
    spread = spread_of(own2)
    sp2[...] = spread
    for copy in halo_sp2:
        copy.start()
    f_b2[...] = (f_im1[...] - h11 * f_b1[...]) * inv2
    f_d2[...] = jscale[0, 0] * f_b2[...] + prolong[0, 0] * spread
    field[...] = apply_local(f_d2[...])
    for copy in halo_e2 + halo_sp2:
        copy.wait_recv()
    back = h11 * inv1
    image = field[...] + apply_link(
        *[(h_e2[side] - back * h_e1[side]) * inv2 + h_prolong[side] * h_sp2[side] for side in (0, 1)]
    )

    row = jnp.zeros((1, NB), F32)
    for i, value in enumerate((total(f_b1[...] * image), total(f_b2[...] * image), total(image * image))):
        row = jnp.where(lane == i, value, row)
    part3[4] = row
    plane3[core] = row
    send_direct(0, 7)
    send_plane3()
    send_direct(7, len(DIRECT))
    g00 = h11 * h11 + h21 * h21
    inv00 = 1.0 / g00
    t0 = beta * h11
    some = None
    for cls in range(4):
        plane3_all(cls).wait_recv()
        first_row = 2 * sum(COUNTS[:cls])
        more = jnp.sum(plane3[first_row : first_row + 2 * COUNTS[cls]], axis=0)
        some = more if some is None else some + more
        part3[cls] = some
        for dz in Z_ORDER:
            if min(6 - hops(dz, NZ), 3) == cls:
                scal_copy(dz).start()
    scal3[z] = some
    direct_all.wait_recv()
    far_sum = jnp.sum(direct[...], axis=0)
    scal_all.wait_recv()
    sums = jnp.sum(scal3[...], axis=0) + far_sum
    h12, h22, energy = [jnp.sum(jnp.where(lane == i, sums, 0.0), axis=1, keepdims=True) for i in range(3)]
    h32 = jnp.sqrt(jnp.maximum(energy - (h12 * h12 + h22 * h22), 0.01 * energy))
    g01 = h11 * h12 + h21 * h22
    g11 = h12 * h12 + h22 * h22 + h32 * h32
    factor = g01 * inv00
    t1 = beta * h12 - factor * t0
    c1 = t1 / (g11 - factor * g01)
    c0 = (t0 - g01 * c1) * inv00
    next_ref[0, 0] = (image - h12 * f_b1[...] - h22 * f_b2[...]) * (1.0 / h32)
    sol_ref[0, 0] = guess[0, 0] + c0 * f_d1[...] + c1 * f_d2[...]

    for copy in halo_guess + halo_send + halo_prolong + halo_e1 + halo_e2 + halo_sp1 + halo_sp2:
        copy.wait_send()
    for which, buf in enumerate((plane1, plane2)):
        for cls in (0, 1):
            plane_all(buf, which, cls).wait_send()
    for cls in range(4):
        plane3_all(cls).wait_send()
    direct_all.wait_send()
    for which, buf in enumerate((line1, line2)):
        for dz in Z_ORDER:
            line_copy(buf, dz, which).wait_send()
        handed_over(buf, which).wait_send()
    scal_all.wait_send()


def on_device(*args):
    field = (BS, NB)
    hbm_spec = pl.BlockSpec(memory_space=pltpu.HBM)
    vmem_spec = pl.BlockSpec(memory_space=pltpu.VMEM)
    sides = (2, BS, NB)
    shape = jax.ShapeDtypeStruct((1, 1, BS, NB), F32)
    return pl.pallas_call(
        kernel,
        out_shape=(shape, shape),
        in_specs=[hbm_spec] * 12,
        out_specs=(vmem_spec, vmem_spec),
        scratch_shapes=[
            *[pltpu.VMEM(args[i].shape, args[i].dtype) for i in (0, 1, 2, 3, 4, 5, 6, 7, 8, 10, 11)],
            pltpu.VMEM(sides, F32),
            pltpu.VMEM(sides, F32),
            pltpu.VMEM((2, 2, NB), I32),
            pltpu.VMEM(sides, F32),
            pltpu.VMEM(sides, F32),
            pltpu.VMEM((2, 1, NB), F32),
            pltpu.VMEM((2, 1, NB), F32),
            *[pltpu.VMEM((PLANE, NB), F32)] * 2,
            pltpu.VMEM((PLANE, 1, NB), F32),
            pltpu.VMEM((2 * len(DIRECT), 1, NB), F32),
            pltpu.VMEM((5, 1, NB), F32),
            *[pltpu.VMEM((2, NZ, HALF + 1, NB), F32)] * 2,
            pltpu.VMEM((NZ, 1, NB), F32),
            *[pltpu.VMEM((CPD, NB), F32)] * 3,
            pltpu.VMEM((2 * NB, NB), BF16),
            pltpu.VMEM((NC // NB, CPD, NB), F32),
            *[pltpu.VMEM((2, NZ, HALF, NB), F32)] * 2,
            *[pltpu.VMEM(field, F32)] * 9,
            pltpu.VMEM((1, NB), F32),
            pltpu.VMEM((1, NB), F32),
            pltpu.SemaphoreType.DMA((11,)),
            pltpu.SemaphoreType.DMA((7, 2)),
            pltpu.SemaphoreType.DMA((7, 2)),
            pltpu.SemaphoreType.DMA((3, 4)),
            pltpu.SemaphoreType.DMA((3, 4)),
            pltpu.SemaphoreType.DMA((2, NZ)),
            pltpu.SemaphoreType.DMA((2, NZ)),
            pltpu.SemaphoreType.DMA((2,)),
            pltpu.SemaphoreType.DMA((2,)),
            *[pltpu.SemaphoreType.DMA] * 4,
            pltpu.SemaphoreType.REGULAR,
        ],
        compiler_params=pltpu.CompilerParams(
            collective_id=0, has_side_effects=True, vmem_limit_bytes=40 * 1024 * 1024
        ),
    )(*[pltpu.with_memory_space_constraint(a, pltpu.HBM) for a in args])


def solution(mesh):
    return jax.shard_map(
        on_device,
        mesh=mesh,
        in_specs=(
            P("sub", "grp", None, None),
            P("sub", "grp", None, None),
            P("sub", "grp", None, None, None),
            P("sub", "grp", None),
            P("sub", "grp", None, None),
            P("sub", "grp", None, None),
            P("sub", "grp", None),
            P(("sub", "grp")),
            P(("sub", "grp"), None),
            P("sub", "grp", None, None),
            P("sub", "grp", None, None),
            P("sub", "grp", None),
        ),
        out_specs=(P("sub", "grp", None, None), P("sub", "grp", None, None)),
        check_vma=False,
    )
```

```python
import jax
import jax.numpy as jnp
from jax import lax
from jax.experimental import pallas as pl
from jax.experimental.pallas import tpu as pltpu
from jax.sharding import PartitionSpec as P

F32 = jnp.float32
BF16 = jnp.bfloat16
I32 = jnp.int32
MESH = pl.DeviceIdType.MESH

BS, NB, CPD = 64, 128, 48
NY, NZ, NG = 8, 12, 8
NSUB = NY * NZ
PLANE = NY * NG
NC = NSUB * NG * CPD
NEAR = (0, 1, 2, 7)
HALF = 12
REACH = {6: 3, 5: 4, 4: 5}


def hops(n, size):
    n %= size
    return min(n, size - n)


CHIPS = sorted(((ox, oy) for ox in range(4) for oy in range(NY)), key=lambda o: hops(o[0], 4) + hops(o[1], NY))
COUNTS = [20, 7, 4, 1]
DIRECT = sorted(
    (
        (hops(ox, 4) + hops(oy, NY) + hops(oz, NZ), ox, oy, oz)
        for ox, oy in CHIPS
        for oz in range(NZ)
        if hops(ox, 4) + hops(oy, NY) > REACH.get(hops(oz, NZ), 6)
    ),
    reverse=True,
)
Z_ORDER = (6, 5, 7, 4, 8, 3, 9, 2, 10, 1, 11)


def iota(shape, dim):
    return lax.broadcasted_iota(I32, shape, dim)


def total(x):
    return jnp.sum(jnp.sum(x, axis=0, keepdims=True), axis=1, keepdims=True)


def kernel(
    rhs_h, guess_h, blocks_h, valve_h, jscale_h, prolong_h, agg_h, cdiag_h, coff_h, send_h, recv_h, live_h,
    out_ref,
    rhs, guess, blocks, valve, jscale, prolong, agg, cdiag, coff, recv, live,
    h_guess, h_prolong, h_send, h_e1, h_e2, h_sp1, h_sp2,
    plane1, plane2, plane3, direct, part3, line1, line2, scal3,
    onehot, place, diag, link, wide, xs, cs, field, out_l, f_b1, f_d1, f_im1, f_b2, f_d2, e1, e2, sp1, sp2,
    load_sem, hs_sem, hr_sem, ps_sem, pr_sem, ls_sem, lr_sem, fs_sem, fr_sem, cs_sem, cr_sem, ds_sem, dr_sem, sync,
):
    s = lax.axis_index("sub")
    g = lax.axis_index("grp")
    y = s // NZ
    z = s % NZ
    me = g * NY + y
    mine = NY * g + 2
    core = g % 2
    sibling = {"grp": g + 1 - 2 * core}
    up = {"sub": (s + 1) % NSUB}
    down = {"sub": (s + NSUB - 1) % NSUB}

    def plane_dev(t):
        return {"sub": (t % NY) * NZ + z, "grp": t // NY}

    def line_dev(dz):
        return {"sub": y * NZ + (z + dz) % NZ}

    barrier = pltpu.get_barrier_semaphore()

    def greet(where):
        pl.semaphore_signal(barrier, inc=1, device_id=where, device_id_type=MESH)

    for where in (up, down):
        greet({**where, "grp": g + 1 - core})

    @pl.when(core == 0)
    def _():
        greet(sibling)

    def greet_plane(t, carry):
        greet({"sub": ((y + t // 4) % NY) * NZ + z, "grp": ((g // 2 + t) % 4) * 2})
        return carry

    def greet_line(i, carry):
        greet({"sub": y * NZ + (z + i) % NZ, "grp": g - core})
        return carry

    lax.fori_loop(16, 32, greet_plane, 0)
    lax.fori_loop(1, NZ, greet_line, 0)
    lax.fori_loop(1, 16, greet_plane, 0)

    @pl.when(core == 1)
    def _():
        greet(sibling)

    loads = [
        pltpu.make_async_copy(src, dst, load_sem.at[i])
        for i, (src, dst) in enumerate(
            (
                (guess_h, guess), (blocks_h, blocks), (rhs_h, rhs), (valve_h, valve), (prolong_h, prolong),
                (agg_h, agg), (recv_h, recv), (live_h, live), (jscale_h, jscale), (cdiag_h, cdiag), (coff_h, coff),
            )
        )
    ]
    for load in loads:
        load.start()

    loads[0].wait()
    loads[4].wait()

    @pl.when(core == 1)
    def _():
        pl.semaphore_wait(barrier, 5)
        pl.semaphore_signal(sync, inc=1, device_id=sibling, device_id_type=MESH)

    @pl.when(core == 0)
    def _():
        pl.semaphore_wait(sync, 1)

    def halo(which, src, dst):
        return [
            pltpu.make_async_remote_copy(
                src, dst.at[side], hs_sem.at[which, side], hr_sem.at[which, side],
                device_id=where, device_id_type=MESH,
            )
            for side, where in ((0, up), (1, down))
        ]

    halo_guess = halo(0, guess.at[0, 0], h_guess)
    halo_send = halo(1, send_h.at[0, 0], h_send)
    halo_prolong = halo(2, prolong.at[0, 0], h_prolong)
    halo_e1 = halo(3, e1, h_e1)
    halo_e2 = halo(4, e2, h_e2)
    halo_sp1 = halo(5, sp1, h_sp1)
    halo_sp2 = halo(6, sp2, h_sp2)
    for copy in halo_send + halo_guess + halo_prolong:
        copy.start()

    def across_plane(buf, which):
        for oy in (4, 3, 5, 2, 6, 1, 7, 0):
            cls = 0 if oy in NEAR else 1

            def one(i, carry):
                pltpu.make_async_remote_copy(
                    buf.at[pl.ds(mine, 1)], buf.at[pl.ds(NY * g + (2 - oy) % NY, 1)],
                    ps_sem.at[which, cls], pr_sem.at[which, cls],
                    device_id={"sub": ((y + oy) % NY) * NZ + z, "grp": (g + i) % NG}, device_id_type=MESH,
                ).start()
                return carry

            lax.fori_loop(4, NG, one, 0)
            lax.fori_loop(0 if oy else 1, 4, one, 0)

    def plane_all(buf, which, cls):
        count = NG * 4 - 1 if cls == 0 else NG * 4
        return pltpu.make_async_remote_copy(
            buf.at[pl.ds(0, count)], buf.at[pl.ds(0, count)], ps_sem.at[which, cls], pr_sem.at[which, cls],
            device_id=up, device_id_type=MESH,
        )

    def line_copy(buf, dz, which):
        return pltpu.make_async_remote_copy(
            buf.at[core, z], buf.at[core, z], ls_sem.at[which, dz], lr_sem.at[which, dz],
            device_id=line_dev(dz), device_id_type=MESH,
        )

    def hand_over(buf, dz, which):
        at = (z + NZ - dz) % NZ
        return pltpu.make_async_remote_copy(
            buf.at[core, at], buf.at[core, at], fs_sem.at[which], fr_sem.at[which],
            device_id=sibling, device_id_type=MESH,
        )

    def handed_over(buf, which):
        return pltpu.make_async_remote_copy(
            buf.at[0, pl.ds(0, NZ - 1)], buf.at[0, pl.ds(0, NZ - 1)], fs_sem.at[which], fr_sem.at[which],
            device_id=sibling, device_id_type=MESH,
        )

    def scal_copy(dz):
        cls = max(6 - hops(dz, NZ), 0)
        return pltpu.make_async_remote_copy(
            part3.at[min(cls, 3)], scal3.at[z], cs_sem, cr_sem, device_id=line_dev(dz), device_id_type=MESH,
        )

    def send_direct(first, last):
        for at in range(first, last):
            _, ox, oy, oz = DIRECT[at]
            for flip in (0, 1):
                pltpu.make_async_remote_copy(
                    part3.at[4], direct.at[2 * at + core], ds_sem, dr_sem,
                    device_id={
                        "sub": ((y + oy) % NY) * NZ + (z + oz) % NZ,
                        "grp": ((g // 2 + ox) % 4) * 2 + (core + flip) % 2,
                    },
                    device_id_type=MESH,
                ).start()

    def send_plane3(chips):
        for at in chips:
            ox, oy = CHIPS[at]
            cls = sum(at >= sum(COUNTS[: i + 1]) for i in range(3))
            for flip in (0, 1):
                if at or flip:
                    pltpu.make_async_remote_copy(
                        part3.at[4], plane3.at[2 * at + core], ps_sem.at[2, cls], pr_sem.at[2, cls],
                        device_id={
                            "sub": ((y + oy) % NY) * NZ + z,
                            "grp": ((g // 2 + ox) % 4) * 2 + (core + flip) % 2,
                        },
                        device_id_type=MESH,
                    ).start()

    def plane3_all(cls):
        count = 2 * COUNTS[cls] - (cls == 0)
        return pltpu.make_async_remote_copy(
            plane3.at[pl.ds(0, count)], plane3.at[pl.ds(0, count)], ps_sem.at[2, cls], pr_sem.at[2, cls],
            device_id=up, device_id_type=MESH,
        )

    direct_all = pltpu.make_async_remote_copy(
        direct, direct, ds_sem, dr_sem, device_id=up, device_id_type=MESH,
    )

    scal_all = pltpu.make_async_remote_copy(
        scal3.at[pl.ds(0, NZ - 1)], scal3.at[pl.ds(0, NZ - 1)], cs_sem, cr_sem, device_id=up, device_id_type=MESH,
    )

    lane = iota((1, NB), 1)
    spare = (CPD * (g + 1)) & (NB - 1)

    def apply_local(v):
        def body(t, carry):
            rows = []
            for i in range(8):
                prod = blocks[0, 0, 8 * t + i].astype(F32) * v
                acc = prod[0:8]
                for j in range(1, 8):
                    acc = acc + prod[8 * j : 8 * j + 8]
                rows.append(jnp.sum(acc, axis=0, keepdims=True))
            out_l[pl.ds(pl.multiple_of(8 * t, 8), 8), :] = jnp.concatenate(rows, axis=0)
            return carry

        lax.fori_loop(0, BS // 8, body, 0)
        return out_l[...] + (3.0 * valve[0].astype(F32)) * v

    def apply_link(below, above):
        both = jnp.concatenate([below, above], axis=1)
        hi = both.astype(BF16)
        lo = (both - hi.astype(F32)).astype(BF16)
        out = jnp.dot(jnp.concatenate([hi, lo], axis=0), link[...], preferred_element_type=F32)
        return out[:BS] + out[BS:]

    def restrict(v):
        weighted = jnp.sum(prolong[0, 0] * v, axis=0, keepdims=True)
        return jnp.sum(onehot[...] * weighted, axis=1, keepdims=True)

    def message(column, scalars):
        row = jnp.sum(place[...] * column, axis=0, keepdims=True)
        for i, value in enumerate(scalars):
            row = jnp.where(lane == spare + i, value, row)
        return row

    def pick(plane, first_row, count):
        spot = iota((count, NB), 1)
        parts = [None] * 3
        extra = None
        for gg in range(NG):
            v = plane[NY * gg + first_row : NY * gg + first_row + count, :]
            for k in range(3):
                lo, hi = max(CPD * gg, NB * k), min(CPD * gg + CPD, NB * k + NB)
                if lo < hi:
                    term = jnp.where((spot >= lo - NB * k) & (spot < hi - NB * k), v, 0.0)
                    parts[k] = term if parts[k] is None else parts[k] + term
            at = (CPD * (gg + 1)) % NB
            term = jnp.where((spot == at) | (spot == at + 1), v, 0.0)
            extra = term if extra is None else extra + term
        return parts, jnp.sum(extra, axis=0, keepdims=True)

    def gather(plane, line, which):
        def send_own():
            for dz in Z_ORDER:
                line_copy(line, dz, which).start()

        plane_all(plane, which, 0).wait_recv()
        parts, some = pick(plane, 0, 4)
        for k in range(3):
            line[0, z, 4 * k : 4 * k + 4, :] = parts[k]
        line[0, z, HALF : HALF + 1, :] = jnp.zeros((1, NB), F32)
        pl.when(core == 0)(send_own)
        plane_all(plane, which, 1).wait_recv()
        parts, rest = pick(plane, 4, 4)
        for k in range(3):
            line[1, z, 4 * k : 4 * k + 4, :] = parts[k]
        line[1, z, HALF : HALF + 1, :] = some + rest
        pl.when(core == 1)(send_own)
        for dz in reversed(Z_ORDER):
            line_copy(line, dz, which).wait_recv()
            hand_over(line, dz, which).start()
        handed_over(line, which).wait_recv()
        sums = jnp.sum(line[1, :, HALF, :], axis=0, keepdims=True)
        return [jnp.sum(jnp.where(lane & 15 == i, sums, 0.0), axis=1, keepdims=True) for i in (0, 1)]

    def coarse_product():
        def body(zz, acc):
            for r in range(NY):
                base = (((y + r + NY - 2) % NY) * NZ + zz) * 3
                for k in range(3):
                    row = 4 * k + r % 4
                    acc = acc + wide[base + k] * xs[r // 4, zz, row : row + 1, :]
            return acc

        acc = lax.fori_loop(0, NZ, body, jnp.zeros((CPD, NB), F32))
        return jnp.sum(acc, axis=1, keepdims=True)

    def spread_of(column):
        sol = diag[:, 0:1] * column + coarse_product()
        return jnp.sum(onehot[...] * sol, axis=0, keepdims=True)

    loads[1].wait()
    loads[3].wait()
    field[...] = apply_local(guess[0, 0])
    for i in (2, 5, 6, 7, 8, 9):
        loads[i].wait()
    onehot[...] = jnp.where(iota((CPD, NB), 0) == agg[0], 1.0, 0.0)
    place[...] = jnp.where(iota((CPD, NB), 1) == (iota((CPD, NB), 0) + CPD * g) & (NB - 1), 1.0, 0.0)
    eye = iota((CPD, CPD), 0) == iota((CPD, CPD), 1)
    diag[...] = jnp.zeros((CPD, NB), F32) + jnp.sum(
        jnp.where(eye, cdiag[...].reshape(1, CPD), 0.0), axis=1, keepdims=True
    )
    rows_i = iota((NB, NB), 0)
    puts = []
    for side in (0, 1):
        alive = iota((NB, NB), 1) < live[0][:, side : side + 1]
        gain = jnp.where(s == (0 if side == 0 else NSUB - 1), 0.0, -0.5)
        puts.append(jnp.where((rows_i == recv[0, 0][side : side + 1, :]) & alive, gain, 0.0).astype(BF16))
    for copy in halo_send:
        copy.wait_recv()
    for side in (0, 1):
        took = jnp.where(rows_i == h_send[side][side : side + 1, :], 1.0, 0.0).astype(BF16)
        both = lax.dot_general(took, puts[side], (((1,), (1,)), ((), ())), preferred_element_type=F32)
        link[NB * side : NB * side + NB, :] = both.astype(BF16)

    @pl.when(core == 0)
    def _():
        pl.semaphore_wait(barrier, PLANE - 1 + 2 * (NZ - 1))
        pl.semaphore_signal(sync, inc=1, device_id=sibling, device_id_type=MESH)

    for copy in halo_guess:
        copy.wait_recv()
    first = rhs[0, 0] - field[...] - apply_link(h_guess[0], h_guess[1])
    own1 = restrict(first)
    plane1[pl.ds(mine, 1), :] = message(own1, [total(first * first), jnp.zeros((1, 1), F32)])

    @pl.when(core == 1)
    def _():
        pl.semaphore_wait(sync, 1)

    across_plane(plane1, 0)
    e1[...] = jscale[0, 0] * first
    for copy in halo_e1:
        copy.start()
    f_b1[...] = first
    loads[10].wait()

    def widen(i, carry):
        for j in range(8):
            at = pl.multiple_of((i * 8 + j) * NB, NB)
            wide[i * 8 + j] = coff[:, pl.ds(at, NB)].astype(F32)
        return carry

    lax.fori_loop(0, NC // (8 * NB), widen, 0)

    square, _ = gather(plane1, line1, 0)
    beta = jnp.sqrt(square)
    inv1 = 1.0 / beta
    for zz in range(NZ):
        for half in (0, 1):
            x = line1[half, zz, 0:HALF, :] * inv1
            cs[half, zz] = x
            xs[half, zz] = x.astype(BF16).astype(F32)
    own1 = own1 * inv1
    spread = spread_of(own1)
    sp1[...] = spread
    for copy in halo_sp1:
        copy.start()
    f_b1[...] = f_b1[...] * inv1
    f_d1[...] = jscale[0, 0] * f_b1[...] + prolong[0, 0] * spread
    field[...] = apply_local(f_d1[...])
    for copy in halo_prolong + halo_e1 + halo_sp1:
        copy.wait_recv()
    image = field[...] + apply_link(
        *[h_e1[side] * inv1 + h_prolong[side] * h_sp1[side] for side in (0, 1)]
    )
    own2 = restrict(image)
    plane2[pl.ds(mine, 1), :] = message(own2, [total(f_b1[...] * image), total(image * image)])
    across_plane(plane2, 1)
    e2[...] = jscale[0, 0] * image
    for copy in halo_e2:
        copy.start()
    f_im1[...] = image

    h11, energy = gather(plane2, line2, 1)
    h21 = jnp.sqrt(jnp.maximum(energy - h11 * h11, 0.01 * energy))
    inv2 = 1.0 / h21
    for zz in range(NZ):
        for half in (0, 1):
            x = (line2[half, zz, 0:HALF, :] - h11 * cs[half, zz]) * inv2
            xs[half, zz] = x.astype(BF16).astype(F32)
    own2 = (own2 - h11 * own1) * inv2
    spread = spread_of(own2)
    sp2[...] = spread
    for copy in halo_sp2:
        copy.start()
    f_b2[...] = (f_im1[...] - h11 * f_b1[...]) * inv2
    f_d2[...] = jscale[0, 0] * f_b2[...] + prolong[0, 0] * spread
    field[...] = apply_local(f_d2[...])
    for copy in halo_e2 + halo_sp2:
        copy.wait_recv()
    back = h11 * inv1
    image = field[...] + apply_link(
        *[(h_e2[side] - back * h_e1[side]) * inv2 + h_prolong[side] * h_sp2[side] for side in (0, 1)]
    )

    row = jnp.zeros((1, NB), F32)
    for i, value in enumerate((total(f_b1[...] * image), total(f_b2[...] * image), total(image * image))):
        row = jnp.where(lane == i, value, row)
    part3[4] = row
    plane3[core] = row
    send_direct(0, 1)
    send_plane3((31, 30, 29, 28, 27))
    send_plane3(range(12, 27))
    send_direct(1, 7)
    send_plane3(reversed(range(12)))
    send_direct(7, len(DIRECT))
    g00 = h11 * h11 + h21 * h21
    inv00 = 1.0 / g00
    t0 = beta * h11
    some = None
    for cls in range(4):
        plane3_all(cls).wait_recv()
        first_row = 2 * sum(COUNTS[:cls])
        more = jnp.sum(plane3[first_row : first_row + 2 * COUNTS[cls]], axis=0)
        some = more if some is None else some + more
        part3[cls] = some
        for dz in Z_ORDER:
            if min(6 - hops(dz, NZ), 3) == cls:
                scal_copy(dz).start()
    scal3[z] = some
    direct_all.wait_recv()
    far_sum = jnp.sum(direct[...], axis=0)
    scal_all.wait_recv()
    sums = jnp.sum(scal3[...], axis=0) + far_sum
    h12, h22, energy = [jnp.sum(jnp.where(lane == i, sums, 0.0), axis=1, keepdims=True) for i in range(3)]
    h32 = jnp.sqrt(jnp.maximum(energy - (h12 * h12 + h22 * h22), 0.01 * energy))
    g01 = h11 * h12 + h21 * h22
    g11 = h12 * h12 + h22 * h22 + h32 * h32
    factor = g01 * inv00
    t1 = beta * h12 - factor * t0
    c1 = t1 / (g11 - factor * g01)
    c0 = (t0 - g01 * c1) * inv00
    out_ref[1, 0, 0] = (image - h12 * f_b1[...] - h22 * f_b2[...]) * (1.0 / h32)
    out_ref[0, 0, 0] = guess[0, 0] + c0 * f_d1[...] + c1 * f_d2[...]

    for copy in halo_guess + halo_send + halo_prolong + halo_e1 + halo_e2 + halo_sp1 + halo_sp2:
        copy.wait_send()
    for which, buf in enumerate((plane1, plane2)):
        for cls in (0, 1):
            plane_all(buf, which, cls).wait_send()
    for cls in range(4):
        plane3_all(cls).wait_send()
    direct_all.wait_send()
    for which, buf in enumerate((line1, line2)):
        for dz in Z_ORDER:
            line_copy(buf, dz, which).wait_send()
        handed_over(buf, which).wait_send()
    scal_all.wait_send()


def on_device(*args):
    field = (BS, NB)
    hbm_spec = pl.BlockSpec(memory_space=pltpu.HBM)
    vmem_spec = pl.BlockSpec(memory_space=pltpu.VMEM)
    sides = (2, BS, NB)
    both = pl.pallas_call(
        kernel,
        out_shape=jax.ShapeDtypeStruct((2, 1, 1, BS, NB), F32),
        in_specs=[hbm_spec] * 12,
        out_specs=vmem_spec,
        scratch_shapes=[
            *[pltpu.VMEM(args[i].shape, args[i].dtype) for i in (0, 1, 2, 3, 4, 5, 6, 7, 8, 10, 11)],
            pltpu.VMEM(sides, F32),
            pltpu.VMEM(sides, F32),
            pltpu.VMEM((2, 2, NB), I32),
            pltpu.VMEM(sides, F32),
            pltpu.VMEM(sides, F32),
            pltpu.VMEM((2, 1, NB), F32),
            pltpu.VMEM((2, 1, NB), F32),
            *[pltpu.VMEM((PLANE, NB), F32)] * 2,
            pltpu.VMEM((PLANE, 1, NB), F32),
            pltpu.VMEM((2 * len(DIRECT), 1, NB), F32),
            pltpu.VMEM((5, 1, NB), F32),
            *[pltpu.VMEM((2, NZ, HALF + 1, NB), F32)] * 2,
            pltpu.VMEM((NZ, 1, NB), F32),
            *[pltpu.VMEM((CPD, NB), F32)] * 3,
            pltpu.VMEM((2 * NB, NB), BF16),
            pltpu.VMEM((NC // NB, CPD, NB), F32),
            *[pltpu.VMEM((2, NZ, HALF, NB), F32)] * 2,
            *[pltpu.VMEM(field, F32)] * 9,
            pltpu.VMEM((1, NB), F32),
            pltpu.VMEM((1, NB), F32),
            pltpu.SemaphoreType.DMA((11,)),
            pltpu.SemaphoreType.DMA((7, 2)),
            pltpu.SemaphoreType.DMA((7, 2)),
            pltpu.SemaphoreType.DMA((3, 4)),
            pltpu.SemaphoreType.DMA((3, 4)),
            pltpu.SemaphoreType.DMA((2, NZ)),
            pltpu.SemaphoreType.DMA((2, NZ)),
            pltpu.SemaphoreType.DMA((2,)),
            pltpu.SemaphoreType.DMA((2,)),
            *[pltpu.SemaphoreType.DMA] * 4,
            pltpu.SemaphoreType.REGULAR,
        ],
        compiler_params=pltpu.CompilerParams(
            collective_id=0, has_side_effects=True, vmem_limit_bytes=40 * 1024 * 1024
        ),
    )(*[pltpu.with_memory_space_constraint(a, pltpu.HBM) for a in args])
    return both[0], both[1]


def solution(mesh):
    return jax.shard_map(
        on_device,
        mesh=mesh,
        in_specs=(
            P("sub", "grp", None, None),
            P("sub", "grp", None, None),
            P("sub", "grp", None, None, None),
            P("sub", "grp", None),
            P("sub", "grp", None, None),
            P("sub", "grp", None, None),
            P("sub", "grp", None),
            P(("sub", "grp")),
            P(("sub", "grp"), None),
            P("sub", "grp", None, None),
            P("sub", "grp", None, None),
            P("sub", "grp", None),
        ),
        out_specs=(P("sub", "grp", None, None), P("sub", "grp", None, None)),
        check_vma=False,
    )
```
